256 devices in a mesh: row: 8 (over x, core), col: 32 (over z, y).
Axes of the slice: x: 4, y: 4, z: 8, core: 2. Of those that a mesh axis runs over, the one named last changes fastest.
Arguments:
- source_pcs: bfloat16 [32768, 64], P('row'), may hold values from -8 to 8
- target_pcs: bfloat16 [131072, 64], P('col'), may hold values from -8 to 8
- source_mass: float32 [32768], P('row'), may hold values from 0.25 to 4
- target_mass: float32 [131072], P('col'), may hold values from 0.25 to 4
- source_scaling: float32 [32768], P('row'), may hold values from 0.1 to 10
- labels: int32 [131072], P('col'), may hold values from 0 to 31
Outputs:
- fates: float32 [32768, 32], P(('row', 'col'))
- source_potential: float32 [32768], P(('row', 'col'))
- target_potential: float32 [131072], P('col')
The draws below stay inside these ranges and needn't reach their ends.
All inputs are finite; a program needn't handle non-finite values.
Results may differ from the reference program's by a relative error of at most 0.00035.
Values may be sent and summed in bfloat16 or wider, within the bound.
No kernel may reach another device: no remote copies, remote signals or barrier semaphores. Data moves between devices by JAX's collectives and lax.ppermute only.
A program may use at most 128 MiB of HBM per device.

```python
import math
import jax
import jax.numpy as jnp
from jax import lax

PCS = 64
SETS = 32
ITERS = 2
NS = 32768
NT = 131072


def cell_cloud(key, cell_key, cell_count):
    subkeys = jax.random.split(cell_key, 2)
    position = jnp.arange(cell_count, dtype=jnp.float32) / (cell_count - 1)
    rising = jnp.sqrt(1.0 + 2.0 * position)[:, None]
    spread = jnp.exp(jax.random.uniform(subkeys[1], (cell_count, 1), minval=-1.2, maxval=1.2))
    values_drawn = jax.random.normal(subkeys[0], (cell_count, PCS))
    return jnp.clip(values_drawn * rising * spread, -8.0, 8.0).astype(jnp.float32)


def draw_source_pcs(key, part):
    return cell_cloud(key, jax.random.fold_in(key, 11), NS).astype(jnp.bfloat16)


def draw_target_pcs(key, part):
    return cell_cloud(key, jax.random.fold_in(key, 23), NT).astype(jnp.bfloat16)


def plant(values, own_key, least, top_value):
    longest = values.shape.index(max(values.shape))
    spots = []
    for shift in (0, 1):
        where = [jax.random.randint(jax.random.fold_in(own_key, axis), (), 0, length) for axis, length in enumerate(values.shape)]
        where[longest] = (where[longest] + shift) % values.shape[longest]
        spots.append(tuple(where))
    return values.at[spots[0]].set(least).at[spots[1]].set(top_value)


def block_levels(rng, shape, cuts, least, top_value):
    gain = 1.0
    for dim, shards_of in cuts:
        heights = jax.random.uniform(jax.random.fold_in(jax.random.fold_in(rng, 6), dim), (shards_of,), jnp.float32, least / len(cuts), top_value / len(cuts))
        gain = gain * jnp.repeat(jnp.exp(heights), shape[dim] // shards_of).reshape((-1,) + (1,) * (len(shape) - 1 - dim))
    return gain


def setup_inputs(seed: int = 0) -> dict:
    arg_keys = jax.random.split(jax.random.key(seed), 7)
    source_pcs = draw_source_pcs(jax.random.fold_in(arg_keys[6], 71), 0)
    target_pcs = draw_target_pcs(jax.random.fold_in(arg_keys[6], 71), 0)
    source_mass = jnp.clip(jnp.exp(math.log(4.0) - 2.7725887 * jax.random.uniform(arg_keys[2], (NS,), jnp.float32) ** block_levels(arg_keys[2], (NS,), ((0, 8),), -0.2, 0.2)), 0.25, 4.0)
    target_mass = jnp.clip(jnp.exp(math.log(4.0) - 2.7725887 * jax.random.uniform(arg_keys[3], (NT,), jnp.float32) ** block_levels(arg_keys[3], (NT,), ((0, 32),), -0.2, 0.2)), 0.25, 4.0)
    source_scaling = jnp.clip(jnp.exp(math.log(10.0) - 4.6051702 * jax.random.uniform(arg_keys[4], (NS,), jnp.float32) ** block_levels(arg_keys[4], (NS,), ((0, 8),), -0.2, 0.2)), 0.1, 10.0)
    labels = plant(jax.random.randint(arg_keys[5], (NT,), 0, SETS), jax.random.fold_in(arg_keys[5], 1), 0, SETS - 1).astype(jnp.int32)
    return dict(source_pcs=source_pcs, target_pcs=target_pcs, source_mass=source_mass, target_mass=target_mass, source_scaling=source_scaling, labels=labels)


entropy_weight = 0.5
offset_small = 1e-6


def kernel_rows(source_pcs, source_sq, target_pcs, target_sq, inverse, first_row, row_count):
    source_block = lax.dynamic_slice_in_dim(source_pcs, first_row, row_count, 0)
    block_sq = lax.dynamic_slice_in_dim(source_sq, first_row, row_count, 0)
    inner_products = lax.dot_general(source_block, target_pcs, (((1,), (1,)), ((), ())), preferred_element_type=jnp.float32)
    exponent = (block_sq[:, None] + target_sq[None, :] - 2.0 * inner_products) * inverse
    return jnp.exp(-exponent).astype(jnp.bfloat16)


def reference(source_pcs, target_pcs, source_mass, target_mass, source_scaling, labels):
    source_wide = source_pcs.astype(jnp.float32)
    target_wide = target_pcs.astype(jnp.float32)
    source_sq = jnp.sum(source_wide * source_wide, 1)
    target_sq = jnp.sum(target_wide * target_wide, 1)
    mean_square = jnp.mean(source_sq) + jnp.mean(target_sq) - 2.0 * jnp.sum(jnp.mean(source_wide, 0) * jnp.mean(target_wide, 0)) + offset_small
    inverse = 1.0 / (entropy_weight * mean_square)
    block_rows = min(NS, 512)

    def one_block(block_index):
        return kernel_rows(source_pcs, source_sq, target_pcs, target_sq, inverse, block_index * block_rows, block_rows)

    kernel = lax.map(one_block, jnp.arange(NS // block_rows, dtype=jnp.int32)).reshape(NS, NT)
    scaled = source_scaling
    target_scaling = target_mass
    for iteration in range(ITERS):
        target_scaling = target_mass / jnp.dot(scaled.astype(jnp.bfloat16), kernel, preferred_element_type=jnp.float32)
        if iteration + 1 < ITERS:
            scaled = source_mass / jnp.dot(kernel, target_scaling.astype(jnp.bfloat16), preferred_element_type=jnp.float32)
    membership = labels[:, None] == jnp.arange(SETS, dtype=jnp.int32)[None, :]
    probes = jnp.where(membership, target_scaling.astype(jnp.bfloat16)[:, None], jnp.zeros((), jnp.bfloat16)).astype(jnp.bfloat16)
    all_sums = jnp.dot(kernel, probes, preferred_element_type=jnp.float32)
    totals = jnp.sum(all_sums, 1)
    fates = all_sums / totals[:, None]
    source_potential = entropy_weight * jnp.log(source_mass / totals)
    target_potential = entropy_weight * jnp.log(target_scaling)
    return (fates, source_potential, target_potential)
```

```python
import functools

import jax
import jax.numpy as jnp
import numpy as np
from jax import lax
from jax.experimental import pallas as pl
from jax.experimental.pallas import tpu as pltpu
from jax.sharding import PartitionSpec as P

SETS = 32
PCS = 64
LANES = 128
DEPTH = 128
entropy_weight = 0.5
offset_small = 1e-06
LOG2E = 1.4426950408889634
F32 = jnp.float32
BF16 = jnp.bfloat16
NT_DIMS = (((1,), (1,)), ((), ()))
VMEM = pl.BlockSpec(memory_space=pltpu.VMEM)
SMEM = pl.BlockSpec(memory_space=pltpu.SMEM)


def split3(t):
    hi = t.astype(BF16).astype(F32)
    mid = (t - hi).astype(BF16).astype(F32)
    lo = t - hi - mid
    return hi, mid, lo


def prep_kernel(peers, x_ref, y_ref, xa_ref, ya_ref, stats_ref):
    rows = 512
    lane = lax.broadcasted_iota(jnp.int32, (rows, LANES - PCS), 1)
    for which, (in_ref, out_ref) in enumerate(((x_ref, xa_ref), (y_ref, ya_ref))):
        total = jnp.zeros((1, PCS), F32)
        total_sq = jnp.zeros((1, 1), F32)
        for first in range(0, in_ref.shape[0], rows):
            part = in_ref[first : first + rows, :]
            wide = part.astype(F32)
            sq = jnp.sum(wide * wide, 1, keepdims=True)
            total = total + jnp.sum(wide, 0, keepdims=True)
            total_sq = total_sq + jnp.sum(sq, 0, keepdims=True)
            parts = split3(-0.5 * sq)
            base = 3 * which
            extra = jnp.where((lane >= 3 - base) & (lane < 6 - base), 1.0, 0.0)
            for k in range(3):
                extra = jnp.where(lane == base + k, parts[k], extra)
            out_ref[first : first + rows, 0:PCS] = part
            out_ref[first : first + rows, PCS:LANES] = extra.astype(BF16)
        for peer in range(peers):
            stats_ref[peer, which : which + 1, 0:PCS] = total
            stats_ref[peer, which : which + 1, PCS:LANES] = jnp.broadcast_to(
                total_sq, (1, LANES - PCS)
            )


def gen_kernel(peers, weight_x, weight_y, xa_ref, ya_ref, stats_ref, scaling_ref, k_ref, out_ref):
    row_count, col_count = xa_ref.shape[0], ya_ref.shape[0]
    sums = jnp.sum(stats_ref[...], 0)
    mean_x = sums[0:1, :] * weight_x
    mean_y = sums[1:2, :] * weight_y
    lane = lax.broadcasted_iota(jnp.int32, (1, LANES), 1)
    square = jnp.where(lane == PCS, mean_x + mean_y, 0.0)
    cross = jnp.where(lane < PCS, mean_x * mean_y, 0.0)
    mean_square = jnp.sum(square - 2.0 * cross, 1, keepdims=True) + offset_small
    factor = (2.0 * LOG2E) / (entropy_weight * mean_square)
    block_cols, block_rows = 512, 256

    def one_block(index, carry):
        first = pl.multiple_of(index * block_cols, block_cols)
        acc = None
        for row in range(0, row_count, block_rows):
            inner = lax.dot_general(
                ya_ref[pl.ds(first, block_cols), :],
                xa_ref[row : row + block_rows, :],
                NT_DIMS,
                preferred_element_type=F32,
            )
            value = jnp.exp2(inner * factor)
            k_ref[pl.ds(first, block_cols), row : row + block_rows] = value.astype(BF16)
            for part in range(0, block_rows, LANES):
                at = (row + part) // LANES
                scaled = scaling_ref[at : at + 1, :].astype(BF16).astype(F32)
                term = value[:, part : part + LANES] * scaled
                acc = term if acc is None else acc + term
        for part in range(0, block_cols, LANES):
            line = jnp.sum(acc[part : part + LANES, :].T, 0, keepdims=True)
            for peer in range(peers):
                out_ref[peer, pl.ds(index * (block_cols // LANES) + part // LANES, 1), :] = line
        return carry

    lax.fori_loop(0, col_count // block_cols, one_block, 0)


def spread(ref, values):
    for t in range(values.shape[0]):
        ref[:, t * LANES : (t + 1) * LANES] = jnp.broadcast_to(
            values[t : t + 1, :], (ref.shape[0], LANES)
        ).astype(BF16)


def row_kernel(peers, k_ref, sums_ref, mass_ref, out_ref, left_ref, line_ref):
    spread(left_ref, mass_ref[...] / jnp.sum(sums_ref[...], 0))
    count = k_ref.shape[1]
    block = 512
    for first in range(0, count, block):
        result = jnp.dot(
            left_ref[...], k_ref[:, first : first + block], preferred_element_type=F32
        )
        for part in range(0, block, LANES):
            at = (first + part) // LANES
            line_ref[at : at + 1, :] = result[0:1, part : part + LANES]
    whole = line_ref[...]
    for peer in range(peers):
        out_ref[peer] = whole


def col_kernel(peers, k_ref, sums_ref, mass_ref, out_ref, left_ref, line_ref):
    spread(left_ref, mass_ref[...] / jnp.sum(sums_ref[...], 0))
    count = k_ref.shape[0]
    block = 512
    for first in range(0, count, block):
        result = lax.dot_general(
            left_ref[...],
            k_ref[first : first + block, :],
            NT_DIMS,
            preferred_element_type=F32,
        )
        for part in range(0, block, LANES):
            at = (first + part) // LANES
            line_ref[at : at + 1, :] = result[0:1, part : part + LANES]
    whole = line_ref[...]
    for peer in range(peers):
        out_ref[peer] = whole


def fate_kernel(k_ref, sums_ref, mass_ref, labels_ref, out_ref, potential_ref, left_ref):
    scaling = mass_ref[...] / jnp.sum(sums_ref[...], 0)
    potential_ref[...] = entropy_weight * jnp.log(scaling)
    sets = lax.broadcasted_iota(jnp.int32, (SETS, LANES), 0)
    for t in range(scaling.shape[0]):
        member = labels_ref[t : t + 1, :] == sets
        left_ref[:, t * LANES : (t + 1) * LANES] = jnp.where(
            member, scaling[t : t + 1, :], 0.0
        ).astype(BF16)
    count = k_ref.shape[1]
    block = 512
    for first in range(0, count, block):
        result = jnp.dot(
            left_ref[...], k_ref[:, first : first + block], preferred_element_type=F32
        )
        for part in range(0, block, LANES):
            out_ref[(first + part) // LANES] = result[:, part : part + LANES]


def last_kernel(at_ref, sums_ref, mass_ref, fates_ref, potential_ref):
    sums = jnp.sum(sums_ref[...], 0)
    totals = jnp.sum(sums, 0, keepdims=True)
    fates_ref[...] = (sums / totals).T
    own = mass_ref[pl.ds(at_ref[0], 1), :]
    potential_ref[...] = entropy_weight * jnp.log(own / totals)


def shape(dims, dtype=F32):
    return jax.ShapeDtypeStruct(dims, dtype)


def call(kernel, name, outs, in_specs, scratch=(), limit=24):
    return pl.pallas_call(
        kernel,
        name=name,
        out_shape=outs,
        in_specs=in_specs,
        out_specs=tuple(VMEM for _ in outs) if isinstance(outs, tuple) else VMEM,
        scratch_shapes=scratch,
        compiler_params=pltpu.CompilerParams(vmem_limit_bytes=limit * 2**20),
    )


def diagonal_groups(row_size, col_size):
    groups = []
    for g in range(row_size):
        group = []
        for c in range(col_size):
            x = (g // 2 + c // 4) % (row_size // 2)
            core = (g % 2 + c % 4) % 2
            group.append((x * 2 + core) * col_size + c)
        groups.append(group)
    return groups


def on_device(row_size, col_size, source_pcs, target_pcs, source_mass, target_mass, source_scaling, labels):
    row_count = source_pcs.shape[0]
    col_count = target_pcs.shape[0]
    lines_r, lines_c = row_count // LANES, col_count // LANES
    source_mass = source_mass.reshape(lines_r, LANES)
    target_mass = target_mass.reshape(lines_c, LANES)
    scaling = source_scaling.reshape(lines_r, LANES)
    labels = labels.reshape(lines_c, LANES)

    xa, ya, stats = call(
        functools.partial(prep_kernel, col_size),
        "prep",
        (
            shape((row_count, DEPTH), BF16),
            shape((col_count, DEPTH), BF16),
            shape((col_size, 2, LANES)),
        ),
        [VMEM] * 2,
    )(source_pcs, target_pcs)
    stats = lax.all_to_all(
        stats, ("row", "col"), 0, 0,
        axis_index_groups=diagonal_groups(row_size, col_size), tiled=True,
    )
    repeats = col_size // row_size
    k, sums = call(
        functools.partial(
            gen_kernel,
            row_size,
            1.0 / (repeats * row_count * row_size),
            1.0 / (col_count * col_size),
        ),
        "gen",
        (pltpu.VMEM((col_count, row_count), BF16), shape((row_size, lines_c, LANES))),
        [VMEM] * 4,
    )(xa, ya, stats, scaling)
    k = pltpu.with_memory_space_constraint(k, pltpu.VMEM)
    sums = lax.all_to_all(sums, "row", 0, 0, tiled=True)
    scratch = [pltpu.VMEM((16, col_count), BF16), pltpu.VMEM((lines_r, LANES), F32)]
    sums = call(
        functools.partial(row_kernel, col_size),
        "rows",
        shape((col_size, lines_r, LANES)),
        [VMEM] * 3,
        scratch,
    )(k, sums, target_mass)
    sums = lax.all_to_all(sums, "col", 0, 0, tiled=True)
    scratch = [pltpu.VMEM((16, row_count), BF16), pltpu.VMEM((lines_c, LANES), F32)]
    sums = call(
        functools.partial(col_kernel, row_size),
        "cols",
        shape((row_size, lines_c, LANES)),
        [VMEM] * 3,
        scratch,
    )(k, sums, source_mass)
    sums = lax.all_to_all(sums, "row", 0, 0, tiled=True)
    sums, target_potential = call(
        fate_kernel,
        "fate",
        (shape((lines_r, SETS, LANES)), shape((lines_c, LANES))),
        [VMEM] * 4,
        [pltpu.VMEM((SETS, col_count), BF16)],
    )(k, sums, target_mass, labels)
    sums = lax.all_to_all(sums, "col", 0, 0, tiled=True)
    at = lax.axis_index("col").astype(jnp.int32).reshape(1)
    fates, source_potential = call(
        last_kernel,
        "last",
        (shape((LANES, SETS)), shape((1, LANES))),
        [SMEM, VMEM, VMEM],
    )(at, sums, source_mass)
    return fates, source_potential.reshape(LANES), target_potential.reshape(col_count)


def solution(mesh):
    placed = (P("row", None), P("col", None), P("row"), P("col"), P("row"), P("col"))
    return jax.shard_map(
        functools.partial(on_device, mesh.shape["row"], mesh.shape["col"]),
        mesh=mesh,
        in_specs=placed,
        out_specs=(P(("row", "col"), None), P(("row", "col")), P("col")),
        check_vma=False,
    )
```

```python
import functools

import jax
import jax.numpy as jnp
import numpy as np
from jax import lax
from jax.experimental import pallas as pl
from jax.experimental.pallas import tpu as pltpu
from jax.sharding import PartitionSpec as P

SETS = 32
PCS = 64
LANES = 128
DEPTH = 128
entropy_weight = 0.5
offset_small = 1e-06
LOG2E = 1.4426950408889634
F32 = jnp.float32
BF16 = jnp.bfloat16
NT_DIMS = (((1,), (1,)), ((), ()))
VMEM = pl.BlockSpec(memory_space=pltpu.VMEM)
SMEM = pl.BlockSpec(memory_space=pltpu.SMEM)


def split3(t):
    hi = t.astype(BF16).astype(F32)
    mid = (t - hi).astype(BF16).astype(F32)
    lo = t - hi - mid
    return hi, mid, lo


def stats_kernel(peers, x_ref, y_ref, out_ref):
    for which, in_ref in enumerate((x_ref, y_ref)):
        total = jnp.zeros((PCS, LANES), F32)
        squares = jnp.zeros((PCS, LANES), F32)
        for first in range(0, in_ref.shape[1], LANES):
            wide = in_ref[:, first : first + LANES].astype(F32)
            total = total + wide
            squares = squares + wide * wide
        sq = jnp.sum(squares, 0, keepdims=True)
        rest = jnp.broadcast_to(sq, (LANES - PCS, LANES))
        line = jnp.sum(jnp.concatenate([total, rest], 0).T, 0, keepdims=True)
        for peer in range(peers):
            out_ref[peer, which : which + 1, :] = line


def points_kernel(x_ref, y_ref, xa_ref, ya_ref):
    width = 512
    row = lax.broadcasted_iota(jnp.int32, (16, width), 0)
    for which, (in_ref, out_ref) in enumerate(((x_ref, xa_ref), (y_ref, ya_ref))):
        base = 3 * which
        for first in range(0, in_ref.shape[1], width):
            wide = in_ref[:, first : first + width].astype(F32)
            parts = split3(-0.5 * jnp.sum(wide * wide, 0, keepdims=True))
            extra = jnp.where((row >= 3 - base) & (row < 6 - base), 1.0, 0.0)
            for k in range(3):
                extra = jnp.where(row == base + k, parts[k], extra)
            pad = jnp.zeros((DEPTH - PCS - 16, width), F32)
            whole = jnp.concatenate([wide, extra, pad], 0)
            for part in range(0, width, LANES):
                out_ref[first + part : first + part + LANES, :] = whole[
                    :, part : part + LANES
                ].T.astype(BF16)


def gen_kernel(peers, weight_x, weight_y, xa_ref, ya_ref, stats_ref, scaling_ref, k_ref, out_ref):
    row_count, col_count = xa_ref.shape[0], ya_ref.shape[0]
    sums = jnp.sum(stats_ref[...], 0)
    mean_x = sums[0:1, :] * weight_x
    mean_y = sums[1:2, :] * weight_y
    lane = lax.broadcasted_iota(jnp.int32, (1, LANES), 1)
    square = jnp.where(lane == PCS, mean_x + mean_y, 0.0)
    cross = jnp.where(lane < PCS, mean_x * mean_y, 0.0)
    mean_square = jnp.sum(square - 2.0 * cross, 1, keepdims=True) + offset_small
    factor = (2.0 * LOG2E) / (entropy_weight * mean_square)
    block_cols, block_rows = 1024, 256

    def one_block(index, carry):
        first = pl.multiple_of(index * block_cols, block_cols)
        acc = None
        for row in range(0, row_count, block_rows):
            inner = lax.dot_general(
                ya_ref[pl.ds(first, block_cols), :],
                xa_ref[row : row + block_rows, :],
                NT_DIMS,
                preferred_element_type=F32,
            )
            value = jnp.exp2(inner * factor)
            k_ref[pl.ds(first, block_cols), row : row + block_rows] = value.astype(BF16)
            for part in range(0, block_rows, LANES):
                at = (row + part) // LANES
                scaled = scaling_ref[at : at + 1, :].astype(BF16).astype(F32)
                term = value[:, part : part + LANES] * scaled
                acc = term if acc is None else acc + term
        for part in range(0, block_cols, LANES):
            line = jnp.sum(acc[part : part + LANES, :].T, 0, keepdims=True)
            for peer in range(peers):
                out_ref[peer, pl.ds(index * (block_cols // LANES) + part // LANES, 1), :] = line
        return carry

    lax.fori_loop(0, col_count // block_cols, one_block, 0, unroll=2)


def spread(ref, values):
    for t in range(values.shape[0]):
        ref[:, t * LANES : (t + 1) * LANES] = jnp.broadcast_to(
            values[t : t + 1, :], (ref.shape[0], LANES)
        ).astype(BF16)


def row_kernel(peers, k_ref, sums_ref, mass_ref, out_ref, left_ref, line_ref):
    spread(left_ref, mass_ref[...] / jnp.sum(sums_ref[...], 0))
    count = k_ref.shape[1]
    block = 512
    for first in range(0, count, block):
        result = jnp.dot(
            left_ref[...], k_ref[:, first : first + block], preferred_element_type=F32
        )
        for part in range(0, block, LANES):
            at = (first + part) // LANES
            line_ref[at : at + 1, :] = result[0:1, part : part + LANES]
    whole = line_ref[...].astype(out_ref.dtype)
    for peer in range(peers):
        out_ref[peer] = whole


def col_kernel(peers, k_ref, sums_ref, mass_ref, out_ref, scaling_ref):
    scaling = mass_ref[...] / jnp.sum(sums_ref[...].astype(F32), 0)
    scaling_ref[...] = scaling.astype(BF16).astype(F32)
    block = 256
    for first in range(0, k_ref.shape[0], block):
        acc = None
        for t in range(scaling.shape[0]):
            part = k_ref[first : first + block, t * LANES : (t + 1) * LANES].astype(F32)
            term = part * scaling_ref[t : t + 1, :]
            acc = term if acc is None else acc + term
        for part in range(0, block, LANES):
            line = jnp.sum(acc[part : part + LANES, :].T, 0, keepdims=True)
            at = (first + part) // LANES
            for peer in range(peers):
                out_ref[peer, at : at + 1, :] = line


def fate_kernel(k_ref, sums_ref, mass_ref, labels_ref, out_ref, potential_ref, left_ref):
    scaling = mass_ref[...] / jnp.sum(sums_ref[...], 0)
    potential_ref[...] = entropy_weight * jnp.log(scaling)
    sets = lax.broadcasted_iota(jnp.int32, (SETS, LANES), 0)
    for t in range(scaling.shape[0]):
        member = labels_ref[t : t + 1, :] == sets
        left_ref[:, t * LANES : (t + 1) * LANES] = jnp.where(
            member, scaling[t : t + 1, :], 0.0
        ).astype(BF16)
    count = k_ref.shape[1]
    block = 512
    for first in range(0, count, block):
        result = jnp.dot(
            left_ref[...], k_ref[:, first : first + block], preferred_element_type=F32
        )
        for part in range(0, block, LANES):
            out_ref[(first + part) // LANES] = result[:, part : part + LANES]


def last_kernel(at_ref, sums_ref, mass_ref, fates_ref, potential_ref):
    sums = jnp.sum(sums_ref[...], 0)
    totals = jnp.sum(sums, 0, keepdims=True)
    fates_ref[...] = sums / totals
    own = mass_ref[pl.ds(at_ref[0], 1), :]
    potential_ref[...] = entropy_weight * jnp.log(own / totals)


def shape(dims, dtype=F32):
    return jax.ShapeDtypeStruct(dims, dtype)


def call(kernel, name, outs, in_specs, scratch=(), limit=24):
    return pl.pallas_call(
        kernel,
        name=name,
        out_shape=outs,
        in_specs=in_specs,
        out_specs=tuple(VMEM for _ in outs) if isinstance(outs, tuple) else VMEM,
        scratch_shapes=scratch,
        compiler_params=pltpu.CompilerParams(vmem_limit_bytes=limit * 2**20),
    )


def diagonal_groups(row_size, col_size):
    groups = []
    for g in range(row_size):
        group = []
        for c in range(col_size):
            x = (g // 2 + c // 4) % (row_size // 2)
            core = (g % 2 + c % 4) % 2
            group.append((x * 2 + core) * col_size + c)
        groups.append(group)
    return groups


def on_device(row_size, col_size, source_pcs, target_pcs, source_mass, target_mass, source_scaling, labels):
    row_count = source_pcs.shape[0]
    col_count = target_pcs.shape[0]
    lines_r, lines_c = row_count // LANES, col_count // LANES
    source_mass = source_mass.reshape(lines_r, LANES)
    target_mass = target_mass.reshape(lines_c, LANES)
    scaling = source_scaling.reshape(lines_r, LANES)
    labels = labels.reshape(lines_c, LANES)

    x_lines = pltpu.with_memory_space_constraint(source_pcs.T, pltpu.VMEM)
    y_lines = pltpu.with_memory_space_constraint(target_pcs.T, pltpu.VMEM)
    stats = call(
        functools.partial(stats_kernel, col_size),
        "stats",
        shape((col_size, 2, LANES)),
        [VMEM] * 2,
    )(x_lines, y_lines)
    stats = lax.all_to_all(
        stats, ("row", "col"), 0, 0,
        axis_index_groups=diagonal_groups(row_size, col_size), tiled=True,
    )
    xa, ya = call(
        points_kernel,
        "points",
        (pltpu.VMEM((row_count, DEPTH), BF16), pltpu.VMEM((col_count, DEPTH), BF16)),
        [VMEM] * 2,
    )(x_lines, y_lines)
    xa = pltpu.with_memory_space_constraint(xa, pltpu.VMEM)
    ya = pltpu.with_memory_space_constraint(ya, pltpu.VMEM)
    stats = pltpu.with_memory_space_constraint(stats, pltpu.VMEM)
    repeats = col_size // row_size
    k, sums = call(
        functools.partial(
            gen_kernel,
            row_size,
            1.0 / (repeats * row_count * row_size),
            1.0 / (col_count * col_size),
        ),
        "gen",
        (pltpu.VMEM((col_count, row_count), BF16), shape((row_size, lines_c, LANES))),
        [VMEM] * 4,
    )(xa, ya, stats, scaling)
    k = pltpu.with_memory_space_constraint(k, pltpu.VMEM)
    sums = lax.all_to_all(sums, "row", 0, 0, tiled=True)
    scratch = [pltpu.VMEM((16, col_count), BF16), pltpu.VMEM((lines_r, LANES), F32)]
    sums = call(
        functools.partial(row_kernel, col_size),
        "rows",
        shape((col_size, lines_r, LANES), BF16),
        [VMEM] * 3,
        scratch,
    )(k, sums, target_mass)
    sums = lax.all_to_all(sums, "col", 0, 0, tiled=True)
    scratch = [pltpu.VMEM((lines_r, LANES), F32)]
    sums = call(
        functools.partial(col_kernel, row_size),
        "cols",
        shape((row_size, lines_c, LANES)),
        [VMEM] * 3,
        scratch,
    )(k, sums, source_mass)
    sums = lax.all_to_all(sums, "row", 0, 0, tiled=True)
    sums, target_potential = call(
        fate_kernel,
        "fate",
        (shape((lines_r, SETS, LANES)), shape((lines_c, LANES))),
        [VMEM] * 4,
        [pltpu.VMEM((SETS, col_count), BF16)],
    )(k, sums, target_mass, labels)
    sums = lax.all_to_all(sums, "col", 0, 0, tiled=True)
    at = lax.axis_index("col").astype(jnp.int32).reshape(1)
    fates, source_potential = call(
        last_kernel,
        "last",
        (shape((SETS, LANES)), shape((1, LANES))),
        [SMEM, VMEM, VMEM],
    )(at, sums, source_mass)
    return fates.T, source_potential.reshape(LANES), target_potential.reshape(col_count)


def solution(mesh):
    placed = (P("row", None), P("col", None), P("row"), P("col"), P("row"), P("col"))
    return jax.shard_map(
        functools.partial(on_device, mesh.shape["row"], mesh.shape["col"]),
        mesh=mesh,
        in_specs=placed,
        out_specs=(P(("row", "col"), None), P(("row", "col")), P("col")),
        check_vma=False,
    )
```

```python
import functools

import jax
import jax.numpy as jnp
import numpy as np
from jax import lax
from jax.experimental import pallas as pl
from jax.experimental.pallas import tpu as pltpu
from jax.sharding import PartitionSpec as P

SETS = 32
PCS = 64
LANES = 128
DEPTH = 128
WIRE_ROWS = 40
LEAST_POWER = -111.0
entropy_weight = 0.5
offset_small = 1e-06
LOG2E = 1.4426950408889634
F32 = jnp.float32
BF16 = jnp.bfloat16
NT_DIMS = (((1,), (1,)), ((), ()))
VMEM = pl.BlockSpec(memory_space=pltpu.VMEM)
SMEM = pl.BlockSpec(memory_space=pltpu.SMEM)


def split3(t):
    hi = t.astype(BF16).astype(F32)
    mid = (t - hi).astype(BF16).astype(F32)
    lo = t - hi - mid
    return hi, mid, lo


def stats_kernel(peers, x_hbm, y_hbm, out_ref, x_ref, y_ref, sems):
    copies = [
        pltpu.make_async_copy(x_hbm, x_ref, sems.at[0]),
        pltpu.make_async_copy(y_hbm, y_ref, sems.at[1]),
    ]
    for copy in copies:
        copy.start()
    for which, in_ref in enumerate((x_ref, y_ref)):
        copies[which].wait()
        total = jnp.zeros((PCS, LANES), F32)
        squares = jnp.zeros((PCS, LANES), F32)
        for first in range(0, in_ref.shape[1], LANES):
            wide = in_ref[:, first : first + LANES].astype(F32)
            total = total + wide
            squares = squares + wide * wide
        sq = jnp.sum(squares, 0, keepdims=True)
        rest = jnp.broadcast_to(sq, (LANES - PCS, LANES))
        line = jnp.sum(jnp.concatenate([total, rest], 0).T, 0, keepdims=True)
        for peer in range(peers):
            out_ref[peer, which : which + 1, :] = line


def points_kernel(x_ref, y_ref, xa_ref, ya_ref):
    width = 512
    row = lax.broadcasted_iota(jnp.int32, (16, width), 0)
    for which, (in_ref, out_ref) in enumerate(((x_ref, xa_ref), (y_ref, ya_ref))):
        base = 3 * which
        for first in range(0, in_ref.shape[1], width):
            wide = in_ref[:, first : first + width].astype(F32)
            parts = split3(-0.5 * jnp.sum(wide * wide, 0, keepdims=True))
            extra = jnp.where((row >= 3 - base) & (row < 6 - base), 1.0, 0.0)
            for k in range(3):
                extra = jnp.where(row == base + k, parts[k], extra)
            pad = jnp.zeros((DEPTH - PCS - 16, width), F32)
            whole = jnp.concatenate([wide, extra, pad], 0)
            for part in range(0, width, LANES):
                out_ref[first + part : first + part + LANES, :] = whole[
                    :, part : part + LANES
                ].T.astype(BF16)


def gen_kernel(peers, weight_x, weight_y, xa_ref, ya_ref, stats_ref, scaling_ref, k_ref, out_ref):
    row_count, col_count = xa_ref.shape[0], ya_ref.shape[0]
    sums = jnp.sum(stats_ref[...], 0)
    mean_x = sums[0:1, :] * weight_x
    mean_y = sums[1:2, :] * weight_y
    lane = lax.broadcasted_iota(jnp.int32, (1, LANES), 1)
    square = jnp.where(lane == PCS, mean_x + mean_y, 0.0)
    cross = jnp.where(lane < PCS, mean_x * mean_y, 0.0)
    mean_square = jnp.sum(square - 2.0 * cross, 1, keepdims=True) + offset_small
    factor = (2.0 * LOG2E) / (entropy_weight * mean_square)
    block_cols, block_rows = 1024, 256

    def one_block(index, carry):
        first = pl.multiple_of(index * block_cols, block_cols)
        acc = None
        for row in range(0, row_count, block_rows):
            inner = lax.dot_general(
                ya_ref[pl.ds(first, block_cols), :],
                xa_ref[row : row + block_rows, :],
                NT_DIMS,
                preferred_element_type=F32,
            )
            value = jnp.exp2(inner * factor)
            k_ref[pl.ds(first, block_cols), row : row + block_rows] = value.astype(BF16)
            for part in range(0, block_rows, LANES):
                at = (row + part) // LANES
                scaled = scaling_ref[at : at + 1, :].astype(BF16).astype(F32)
                term = value[:, part : part + LANES] * scaled
                acc = term if acc is None else acc + term
        for part in range(0, block_cols, LANES):
            line = jnp.sum(acc[part : part + LANES, :].T, 0, keepdims=True)
            for peer in range(peers):
                out_ref[peer, pl.ds(index * (block_cols // LANES) + part // LANES, 1), :] = line
        return carry

    lax.fori_loop(0, col_count // block_cols, one_block, 0, unroll=2)


def spread(ref, values):
    for t in range(values.shape[0]):
        ref[:, t * LANES : (t + 1) * LANES] = jnp.broadcast_to(
            values[t : t + 1, :], (ref.shape[0], LANES)
        ).astype(BF16)


def row_kernel(peers, k_ref, sums_ref, mass_ref, out_ref, left_ref, line_ref):
    spread(left_ref, mass_ref[...] / jnp.sum(sums_ref[...], 0))
    count = k_ref.shape[1]
    block = 512
    for first in range(0, count, block):
        result = jnp.dot(
            left_ref[...], k_ref[:, first : first + block], preferred_element_type=F32
        )
        for part in range(0, block, LANES):
            at = (first + part) // LANES
            line_ref[at : at + 1, :] = result[0:1, part : part + LANES]
    whole = line_ref[...].astype(out_ref.dtype)
    for peer in range(peers):
        out_ref[peer] = whole


def col_kernel(peers, k_ref, sums_ref, mass_ref, out_ref, scaling_ref):
    scaling = mass_ref[...] / jnp.sum(sums_ref[...].astype(F32), 0)
    scaling_ref[...] = scaling.astype(BF16).astype(F32)
    block = 256
    for first in range(0, k_ref.shape[0], block):
        acc = None
        for t in range(scaling.shape[0]):
            part = k_ref[first : first + block, t * LANES : (t + 1) * LANES].astype(F32)
            term = part * scaling_ref[t : t + 1, :]
            acc = term if acc is None else acc + term
        for part in range(0, block, LANES):
            line = jnp.sum(acc[part : part + LANES, :].T, 0, keepdims=True)
            at = (first + part) // LANES
            for peer in range(peers):
                out_ref[peer, at : at + 1, :] = line


def fate_kernel(k_ref, sums_ref, mass_ref, labels_ref, out_ref, potential_ref, left_ref):
    scaling = mass_ref[...] / jnp.sum(sums_ref[...], 0)
    potential_ref[...] = entropy_weight * jnp.log(scaling)
    sets = lax.broadcasted_iota(jnp.int32, (SETS, LANES), 0)
    for t in range(scaling.shape[0]):
        member = labels_ref[t : t + 1, :] == sets
        left_ref[:, t * LANES : (t + 1) * LANES] = jnp.where(
            member, scaling[t : t + 1, :], 0.0
        ).astype(BF16)
    count = k_ref.shape[1]
    block = 512
    for first in range(0, count, block):
        result = jnp.dot(
            left_ref[...], k_ref[:, first : first + block], preferred_element_type=F32
        )
        for part in range(0, block, LANES):
            share = result[:, part : part + LANES]
            top = jnp.log2(jnp.max(share, 0, keepdims=True))
            power = jnp.clip(jnp.floor(top) + 1.0, LEAST_POWER, 127.0)
            scaled = jnp.minimum(share * jnp.exp2(15.0 - power) + 0.5, 32767.0)
            rest = jnp.broadcast_to(power, (WIRE_ROWS - SETS, LANES))
            coded = jnp.concatenate([scaled, rest], 0).astype(jnp.int32)
            out_ref[(first + part) // LANES] = coded.astype(jnp.int16)


def last_kernel(at_ref, sums_ref, mass_ref, fates_ref, potential_ref):
    sums = jnp.zeros((SETS, LANES), F32)
    for peer in range(sums_ref.shape[0]):
        coded = sums_ref[peer].astype(jnp.int32).astype(F32)
        sums = sums + coded[0:SETS, :] * jnp.exp2(coded[SETS : SETS + 1, :] - 15.0)
    totals = jnp.sum(sums, 0, keepdims=True)
    fates_ref[...] = sums / totals
    own = mass_ref[pl.ds(at_ref[0], 1), :]
    potential_ref[...] = entropy_weight * jnp.log(own / totals)


def shape(dims, dtype=F32):
    return jax.ShapeDtypeStruct(dims, dtype)


def call(kernel, name, outs, in_specs, scratch=(), limit=24):
    return pl.pallas_call(
        kernel,
        name=name,
        out_shape=outs,
        in_specs=in_specs,
        out_specs=tuple(VMEM for _ in outs) if isinstance(outs, tuple) else VMEM,
        scratch_shapes=scratch,
        compiler_params=pltpu.CompilerParams(vmem_limit_bytes=limit * 2**20),
    )


def diagonal_groups(row_size, col_size):
    groups = []
    for g in range(row_size):
        group = []
        for c in range(col_size):
            x = (g // 2 + c // 4) % (row_size // 2)
            core = (g % 2 + c % 4) % 2
            group.append((x * 2 + core) * col_size + c)
        groups.append(group)
    return groups


def on_device(row_size, col_size, source_pcs, target_pcs, source_mass, target_mass, source_scaling, labels):
    row_count = source_pcs.shape[0]
    col_count = target_pcs.shape[0]
    lines_r, lines_c = row_count // LANES, col_count // LANES
    source_mass = source_mass.reshape(lines_r, LANES)
    target_mass = target_mass.reshape(lines_c, LANES)
    scaling = source_scaling.reshape(lines_r, LANES)
    labels = labels.reshape(lines_c, LANES)

    x_lines, y_lines = source_pcs.T, target_pcs.T
    stats = call(
        functools.partial(stats_kernel, col_size),
        "stats",
        shape((col_size, 2, LANES)),
        [pl.BlockSpec(memory_space=pltpu.HBM)] * 2,
        [
            pltpu.VMEM(x_lines.shape, BF16),
            pltpu.VMEM(y_lines.shape, BF16),
            pltpu.SemaphoreType.DMA((2,)),
        ],
    )(x_lines, y_lines)
    stats = lax.all_to_all(
        stats, ("row", "col"), 0, 0,
        axis_index_groups=diagonal_groups(row_size, col_size), tiled=True,
    )
    xa, ya = call(
        points_kernel,
        "points",
        (pltpu.VMEM((row_count, DEPTH), BF16), pltpu.VMEM((col_count, DEPTH), BF16)),
        [VMEM] * 2,
    )(x_lines, y_lines)
    xa = pltpu.with_memory_space_constraint(xa, pltpu.VMEM)
    ya = pltpu.with_memory_space_constraint(ya, pltpu.VMEM)
    stats = pltpu.with_memory_space_constraint(stats, pltpu.VMEM)
    repeats = col_size // row_size
    k, sums = call(
        functools.partial(
            gen_kernel,
            row_size,
            1.0 / (repeats * row_count * row_size),
            1.0 / (col_count * col_size),
        ),
        "gen",
        (pltpu.VMEM((col_count, row_count), BF16), shape((row_size, lines_c, LANES))),
        [VMEM] * 4,
    )(xa, ya, stats, scaling)
    k = pltpu.with_memory_space_constraint(k, pltpu.VMEM)
    sums = lax.all_to_all(sums, "row", 0, 0, tiled=True)
    scratch = [pltpu.VMEM((16, col_count), BF16), pltpu.VMEM((lines_r, LANES), F32)]
    sums = call(
        functools.partial(row_kernel, col_size),
        "rows",
        shape((col_size, lines_r, LANES), BF16),
        [VMEM] * 3,
        scratch,
    )(k, sums, target_mass)
    sums = lax.all_to_all(sums, "col", 0, 0, tiled=True)
    scratch = [pltpu.VMEM((lines_r, LANES), F32)]
    sums = call(
        functools.partial(col_kernel, row_size),
        "cols",
        shape((row_size, lines_c, LANES)),
        [VMEM] * 3,
        scratch,
    )(k, sums, source_mass)
    sums = lax.all_to_all(sums, "row", 0, 0, tiled=True)
    sums, target_potential = call(
        fate_kernel,
        "fate",
        (shape((lines_r, WIRE_ROWS, LANES), jnp.int16), shape((lines_c, LANES))),
        [VMEM] * 4,
        [pltpu.VMEM((SETS, col_count), BF16)],
    )(k, sums, target_mass, labels)
    sums = lax.all_to_all(sums, "col", 0, 0, tiled=True)
    at = lax.axis_index("col").astype(jnp.int32).reshape(1)
    fates, source_potential = call(
        last_kernel,
        "last",
        (shape((SETS, LANES)), shape((1, LANES))),
        [SMEM, VMEM, VMEM],
    )(at, sums, source_mass)
    return fates.T, source_potential.reshape(LANES), target_potential.reshape(col_count)


def solution(mesh):
    placed = (P("row", None), P("col", None), P("row"), P("col"), P("row"), P("col"))
    return jax.shard_map(
        functools.partial(on_device, mesh.shape["row"], mesh.shape["col"]),
        mesh=mesh,
        in_specs=placed,
        out_specs=(P(("row", "col"), None), P(("row", "col")), P("col")),
        check_vma=False,
    )
```

```python
import functools

import jax
import jax.numpy as jnp
import numpy as np
from jax import lax
from jax.experimental import pallas as pl
from jax.experimental.pallas import tpu as pltpu
from jax.sharding import PartitionSpec as P

SETS = 32
PCS = 64
LANES = 128
DEPTH = 128
WIRE_ROWS = 40
LEAST_POWER = -111.0
entropy_weight = 0.5
offset_small = 1e-06
LOG2E = 1.4426950408889634
F32 = jnp.float32
BF16 = jnp.bfloat16
NT_DIMS = (((1,), (1,)), ((), ()))
VMEM = pl.BlockSpec(memory_space=pltpu.VMEM)
SMEM = pl.BlockSpec(memory_space=pltpu.SMEM)


def split3(t):
    hi = t.astype(BF16).astype(F32)
    mid = (t - hi).astype(BF16).astype(F32)
    lo = t - hi - mid
    return hi, mid, lo


def stats_kernel(peers, x_hbm, y_hbm, out_ref, x_ref, y_ref, sems):
    copies = [
        pltpu.make_async_copy(x_hbm, x_ref, sems.at[0]),
        pltpu.make_async_copy(y_hbm, y_ref, sems.at[1]),
    ]
    for copy in copies:
        copy.start()
    for which, in_ref in enumerate((x_ref, y_ref)):
        copies[which].wait()
        total = jnp.zeros((PCS, LANES), F32)
        squares = jnp.zeros((PCS, LANES), F32)
        for first in range(0, in_ref.shape[1], LANES):
            wide = in_ref[:, first : first + LANES].astype(F32)
            total = total + wide
            squares = squares + wide * wide
        sq = jnp.sum(squares, 0, keepdims=True)
        rest = jnp.broadcast_to(sq, (LANES - PCS, LANES))
        line = jnp.sum(jnp.concatenate([total, rest], 0).T, 0, keepdims=True)
        for peer in range(peers):
            out_ref[peer, which : which + 1, :] = line


def points_kernel(x_ref, y_ref, xa_ref, ya_ref):
    width = 512
    row = lax.broadcasted_iota(jnp.int32, (16, width), 0)
    for which, (in_ref, out_ref) in enumerate(((x_ref, xa_ref), (y_ref, ya_ref))):
        base = 3 * which
        for first in range(0, in_ref.shape[1], width):
            wide = in_ref[:, first : first + width].astype(F32)
            parts = split3(-0.5 * jnp.sum(wide * wide, 0, keepdims=True))
            extra = jnp.where((row >= 3 - base) & (row < 6 - base), 1.0, 0.0)
            for k in range(3):
                extra = jnp.where(row == base + k, parts[k], extra)
            pad = jnp.zeros((DEPTH - PCS - 16, width), F32)
            whole = jnp.concatenate([wide, extra, pad], 0)
            for part in range(0, width, LANES):
                out_ref[first + part : first + part + LANES, :] = whole[
                    :, part : part + LANES
                ].T.astype(BF16)


def gen_kernel(peers, weight_x, weight_y, xa_ref, ya_ref, stats_ref, scaling_ref, k_ref, out_ref, line_ref):
    row_count, col_count = xa_ref.shape[0], ya_ref.shape[0]
    sums = jnp.sum(stats_ref[...], 0)
    mean_x = sums[0:1, :] * weight_x
    mean_y = sums[1:2, :] * weight_y
    lane = lax.broadcasted_iota(jnp.int32, (1, LANES), 1)
    square = jnp.where(lane == PCS, mean_x + mean_y, 0.0)
    cross = jnp.where(lane < PCS, mean_x * mean_y, 0.0)
    mean_square = jnp.sum(square - 2.0 * cross, 1, keepdims=True) + offset_small
    factor = (2.0 * LOG2E) / (entropy_weight * mean_square)
    block_cols, block_rows = 2048, 256

    def one_block(index, carry):
        first = pl.multiple_of(index * block_cols, block_cols)
        acc = None
        for row in range(0, row_count, block_rows):
            inner = lax.dot_general(
                ya_ref[pl.ds(first, block_cols), :],
                xa_ref[row : row + block_rows, :],
                NT_DIMS,
                preferred_element_type=F32,
            )
            value = jnp.exp2(inner * factor)
            k_ref[pl.ds(first, block_cols), row : row + block_rows] = value.astype(BF16)
            for part in range(0, block_rows, LANES):
                at = (row + part) // LANES
                scaled = scaling_ref[at : at + 1, :].astype(BF16).astype(F32)
                term = value[:, part : part + LANES] * scaled
                acc = term if acc is None else acc + term
        for part in range(0, block_cols, LANES):
            line = jnp.sum(acc[part : part + LANES, :].T, 0, keepdims=True)
            line_ref[pl.ds(index * (block_cols // LANES) + part // LANES, 1), :] = line
        return carry

    lax.fori_loop(0, col_count // block_cols, one_block, 0, unroll=2)
    whole = line_ref[...].astype(out_ref.dtype)
    for peer in range(peers):
        out_ref[peer] = whole


def spread(ref, values):
    for t in range(values.shape[0]):
        ref[:, t * LANES : (t + 1) * LANES] = jnp.broadcast_to(
            values[t : t + 1, :], (ref.shape[0], LANES)
        ).astype(BF16)


def row_kernel(peers, k_ref, sums_ref, mass_ref, out_ref, left_ref, line_ref):
    spread(left_ref, mass_ref[...] / jnp.sum(sums_ref[...].astype(F32), 0))
    count = k_ref.shape[1]
    block = 512
    for first in range(0, count, block):
        result = jnp.dot(
            left_ref[...], k_ref[:, first : first + block], preferred_element_type=F32
        )
        for part in range(0, block, LANES):
            at = (first + part) // LANES
            line_ref[at : at + 1, :] = result[0:1, part : part + LANES]
    whole = line_ref[...].astype(out_ref.dtype)
    for peer in range(peers):
        out_ref[peer] = whole


def col_kernel(peers, k_ref, sums_ref, mass_ref, out_ref, scaling_ref):
    scaling = mass_ref[...] / jnp.sum(sums_ref[...].astype(F32), 0)
    scaling_ref[...] = scaling.astype(BF16).astype(F32)
    block = 256
    for first in range(0, k_ref.shape[0], block):
        acc = None
        for t in range(scaling.shape[0]):
            part = k_ref[first : first + block, t * LANES : (t + 1) * LANES].astype(F32)
            term = part * scaling_ref[t : t + 1, :]
            acc = term if acc is None else acc + term
        for part in range(0, block, LANES):
            line = jnp.sum(acc[part : part + LANES, :].T, 0, keepdims=True)
            at = (first + part) // LANES
            for peer in range(peers):
                out_ref[peer, at : at + 1, :] = line


def fate_kernel(k_ref, sums_ref, mass_ref, labels_ref, out_ref, potential_ref, left_ref):
    scaling = mass_ref[...] / jnp.sum(sums_ref[...], 0)
    potential_ref[...] = entropy_weight * jnp.log(scaling)
    sets = lax.broadcasted_iota(jnp.int32, (SETS, LANES), 0)
    for t in range(scaling.shape[0]):
        member = labels_ref[t : t + 1, :] == sets
        left_ref[:, t * LANES : (t + 1) * LANES] = jnp.where(
            member, scaling[t : t + 1, :], 0.0
        ).astype(BF16)
    count = k_ref.shape[1]
    block = 512
    for first in range(0, count, block):
        result = jnp.dot(
            left_ref[...], k_ref[:, first : first + block], preferred_element_type=F32
        )
        for part in range(0, block, LANES):
            share = result[:, part : part + LANES]
            top = jnp.log2(jnp.max(share, 0, keepdims=True))
            power = jnp.clip(jnp.floor(top) + 1.0, LEAST_POWER, 127.0)
            scaled = jnp.minimum(share * jnp.exp2(15.0 - power) + 0.5, 32767.0)
            rest = jnp.broadcast_to(power, (WIRE_ROWS - SETS, LANES))
            coded = jnp.concatenate([scaled, rest], 0).astype(jnp.int32)
            out_ref[(first + part) // LANES] = coded.astype(jnp.int16)


def last_kernel(at_ref, sums_ref, mass_ref, fates_ref, potential_ref):
    sums = jnp.zeros((SETS, LANES), F32)
    for peer in range(sums_ref.shape[0]):
        coded = sums_ref[peer].astype(jnp.int32).astype(F32)
        sums = sums + coded[0:SETS, :] * jnp.exp2(coded[SETS : SETS + 1, :] - 15.0)
    totals = jnp.sum(sums, 0, keepdims=True)
    fates_ref[...] = sums / totals
    own = mass_ref[pl.ds(at_ref[0], 1), :]
    potential_ref[...] = entropy_weight * jnp.log(own / totals)


def shape(dims, dtype=F32):
    return jax.ShapeDtypeStruct(dims, dtype)


def call(kernel, name, outs, in_specs, scratch=(), limit=24):
    return pl.pallas_call(
        kernel,
        name=name,
        out_shape=outs,
        in_specs=in_specs,
        out_specs=tuple(VMEM for _ in outs) if isinstance(outs, tuple) else VMEM,
        scratch_shapes=scratch,
        compiler_params=pltpu.CompilerParams(vmem_limit_bytes=limit * 2**20),
    )


def diagonal_groups(row_size, col_size):
    groups = []
    for g in range(row_size):
        group = []
        for c in range(col_size):
            x = (g // 2 + c // 4) % (row_size // 2)
            core = (g % 2 + c % 4) % 2
            group.append((x * 2 + core) * col_size + c)
        groups.append(group)
    return groups


def on_device(row_size, col_size, source_pcs, target_pcs, source_mass, target_mass, source_scaling, labels):
    row_count = source_pcs.shape[0]
    col_count = target_pcs.shape[0]
    lines_r, lines_c = row_count // LANES, col_count // LANES
    source_mass = source_mass.reshape(lines_r, LANES)
    target_mass = target_mass.reshape(lines_c, LANES)
    scaling = source_scaling.reshape(lines_r, LANES)
    labels = labels.reshape(lines_c, LANES)

    x_lines, y_lines = source_pcs.T, target_pcs.T
    x_far = pltpu.with_memory_space_constraint(x_lines, pltpu.HBM)
    y_far = pltpu.with_memory_space_constraint(y_lines, pltpu.HBM)
    stats = call(
        functools.partial(stats_kernel, col_size),
        "stats",
        shape((col_size, 2, LANES)),
        [pl.BlockSpec(memory_space=pltpu.HBM)] * 2,
        [
            pltpu.VMEM(x_lines.shape, BF16),
            pltpu.VMEM(y_lines.shape, BF16),
            pltpu.SemaphoreType.DMA((2,)),
        ],
    )(x_far, y_far)
    stats = lax.all_to_all(
        stats, ("row", "col"), 0, 0,
        axis_index_groups=diagonal_groups(row_size, col_size), tiled=True,
    )
    xa, ya = call(
        points_kernel,
        "points",
        (pltpu.VMEM((row_count, DEPTH), BF16), pltpu.VMEM((col_count, DEPTH), BF16)),
        [VMEM] * 2,
    )(x_lines, y_lines)
    xa = pltpu.with_memory_space_constraint(xa, pltpu.VMEM)
    ya = pltpu.with_memory_space_constraint(ya, pltpu.VMEM)
    stats = pltpu.with_memory_space_constraint(stats, pltpu.VMEM)
    repeats = col_size // row_size
    k, sums = call(
        functools.partial(
            gen_kernel,
            row_size,
            1.0 / (repeats * row_count * row_size),
            1.0 / (col_count * col_size),
        ),
        "gen",
        (pltpu.VMEM((col_count, row_count), BF16), shape((row_size, lines_c, LANES), BF16)),
        [VMEM] * 4,
        [pltpu.VMEM((lines_c, LANES), F32)],
    )(xa, ya, stats, scaling)
    k = pltpu.with_memory_space_constraint(k, pltpu.VMEM)
    sums = lax.all_to_all(sums, "row", 0, 0, tiled=True)
    scratch = [pltpu.VMEM((16, col_count), BF16), pltpu.VMEM((lines_r, LANES), F32)]
    sums = call(
        functools.partial(row_kernel, col_size),
        "rows",
        shape((col_size, lines_r, LANES), BF16),
        [VMEM] * 3,
        scratch,
    )(k, sums, target_mass)
    sums = lax.all_to_all(sums, "col", 0, 0, tiled=True)
    scratch = [pltpu.VMEM((lines_r, LANES), F32)]
    sums = call(
        functools.partial(col_kernel, row_size),
        "cols",
        shape((row_size, lines_c, LANES)),
        [VMEM] * 3,
        scratch,
    )(k, sums, source_mass)
    sums = lax.all_to_all(sums, "row", 0, 0, tiled=True)
    sums, target_potential = call(
        fate_kernel,
        "fate",
        (shape((lines_r, WIRE_ROWS, LANES), jnp.int16), shape((lines_c, LANES))),
        [VMEM] * 4,
        [pltpu.VMEM((SETS, col_count), BF16)],
    )(k, sums, target_mass, labels)
    sums = lax.all_to_all(sums, "col", 0, 0, tiled=True)
    at = lax.axis_index("col").astype(jnp.int32).reshape(1)
    fates, source_potential = call(
        last_kernel,
        "last",
        (shape((SETS, LANES)), shape((1, LANES))),
        [SMEM, VMEM, VMEM],
    )(at, sums, source_mass)
    return fates.T, source_potential.reshape(LANES), target_potential.reshape(col_count)


def solution(mesh):
    placed = (P("row", None), P("col", None), P("row"), P("col"), P("row"), P("col"))
    return jax.shard_map(
        functools.partial(on_device, mesh.shape["row"], mesh.shape["col"]),
        mesh=mesh,
        in_specs=placed,
        out_specs=(P(("row", "col"), None), P(("row", "col")), P("col")),
        check_vma=False,
    )
```

```python
import functools

import jax
import jax.numpy as jnp
import numpy as np
from jax import lax
from jax.experimental import pallas as pl
from jax.experimental.pallas import tpu as pltpu
from jax.sharding import PartitionSpec as P

SETS = 32
PCS = 64
LANES = 128
DEPTH = 128
WIRE_ROWS = 40
PIECES = 4
LEAST_POWER = -111.0
entropy_weight = 0.5
offset_small = 1e-06
LOG2E = 1.4426950408889634
F32 = jnp.float32
BF16 = jnp.bfloat16
NT_DIMS = (((1,), (1,)), ((), ()))
VMEM = pl.BlockSpec(memory_space=pltpu.VMEM)
HBM = pl.BlockSpec(memory_space=pltpu.HBM)
SMEM = pl.BlockSpec(memory_space=pltpu.SMEM)


def split3(t):
    hi = t.astype(BF16).astype(F32)
    mid = (t - hi).astype(BF16).astype(F32)
    lo = t - hi - mid
    return hi, mid, lo


def stats_kernel(peers, x_hbm, y_hbm, out_ref, x_ref, y_ref, sems):
    width = x_ref.shape[1] // PIECES
    pairs = ((x_hbm, x_ref), (y_hbm, y_ref))

    def piece(which, number):
        columns = pl.ds(number * width, width)
        far, near = pairs[which]
        return pltpu.make_async_copy(
            far.at[:, columns], near.at[:, columns], sems.at[which, number]
        )

    for which in range(2):
        for number in range(PIECES):
            piece(which, number).start()
    for which, in_ref in enumerate((x_ref, y_ref)):
        total = jnp.zeros((PCS, LANES), F32)
        squares = jnp.zeros((PCS, LANES), F32)
        for first in range(0, in_ref.shape[1], LANES):
            if first % width == 0:
                piece(which, first // width).wait()
            wide = in_ref[:, first : first + LANES].astype(F32)
            total = total + wide
            squares = squares + wide * wide
        sq = jnp.sum(squares, 0, keepdims=True)
        rest = jnp.broadcast_to(sq, (LANES - PCS, LANES))
        line = jnp.sum(jnp.concatenate([total, rest], 0).T, 0, keepdims=True)
        for peer in range(peers):
            out_ref[peer, which : which + 1, :] = line


def points_kernel(x_ref, y_ref, xa_ref, ya_ref):
    width = 512
    row = lax.broadcasted_iota(jnp.int32, (16, width), 0)
    for which, (in_ref, out_ref) in enumerate(((x_ref, xa_ref), (y_ref, ya_ref))):
        base = 3 * which
        for first in range(0, in_ref.shape[1], width):
            wide = in_ref[:, first : first + width].astype(F32)
            parts = split3(-0.5 * jnp.sum(wide * wide, 0, keepdims=True))
            extra = jnp.where((row >= 3 - base) & (row < 6 - base), 1.0, 0.0)
            for k in range(3):
                extra = jnp.where(row == base + k, parts[k], extra)
            pad = jnp.zeros((DEPTH - PCS - 16, width), F32)
            whole = jnp.concatenate([wide, extra, pad], 0)
            for part in range(0, width, LANES):
                out_ref[first + part : first + part + LANES, :] = whole[
                    :, part : part + LANES
                ].T.astype(BF16)


def gen_kernel(peers, weight_x, weight_y, xa_ref, ya_ref, stats_ref, scaling_ref, k_ref, out_ref, line_ref):
    row_count, col_count = xa_ref.shape[0], ya_ref.shape[0]
    sums = jnp.sum(stats_ref[...], 0)
    mean_x = sums[0:1, :] * weight_x
    mean_y = sums[1:2, :] * weight_y
    lane = lax.broadcasted_iota(jnp.int32, (1, LANES), 1)
    square = jnp.where(lane == PCS, mean_x + mean_y, 0.0)
    cross = jnp.where(lane < PCS, mean_x * mean_y, 0.0)
    mean_square = jnp.sum(square - 2.0 * cross, 1, keepdims=True) + offset_small
    factor = (2.0 * LOG2E) / (entropy_weight * mean_square)
    block_cols, block_rows = 2048, 256

    def one_block(index, carry):
        first = pl.multiple_of(index * block_cols, block_cols)
        acc = None
        for row in range(0, row_count, block_rows):
            inner = lax.dot_general(
                ya_ref[pl.ds(first, block_cols), :],
                xa_ref[row : row + block_rows, :],
                NT_DIMS,
                preferred_element_type=F32,
            )
            value = jnp.exp2(inner * factor)
            k_ref[pl.ds(first, block_cols), row : row + block_rows] = value.astype(BF16)
            for part in range(0, block_rows, LANES):
                at = (row + part) // LANES
                scaled = scaling_ref[at : at + 1, :].astype(BF16).astype(F32)
                term = value[:, part : part + LANES] * scaled
                acc = term if acc is None else acc + term
        for part in range(0, block_cols, LANES):
            line = jnp.sum(acc[part : part + LANES, :].T, 0, keepdims=True)
            line_ref[pl.ds(index * (block_cols // LANES) + part // LANES, 1), :] = line
        return carry

    lax.fori_loop(0, col_count // block_cols, one_block, 0, unroll=2)
    whole = line_ref[...].astype(out_ref.dtype)
    for peer in range(peers):
        out_ref[peer] = whole


def spread(ref, values):
    for t in range(values.shape[0]):
        ref[:, t * LANES : (t + 1) * LANES] = jnp.broadcast_to(
            values[t : t + 1, :], (ref.shape[0], LANES)
        ).astype(BF16)


def row_kernel(
    peers, k_ref, sums_ref, mass_ref, out_hbm, left_ref, line_ref, whole_ref, sems
):
    spread(left_ref, mass_ref[...] / jnp.sum(sums_ref[...].astype(F32), 0))
    count = k_ref.shape[1]
    block = 512
    for first in range(0, count, block):
        result = jnp.dot(
            left_ref[...], k_ref[:, first : first + block], preferred_element_type=F32
        )
        for part in range(0, block, LANES):
            at = (first + part) // LANES
            line_ref[at : at + 1, :] = result[0:1, part : part + LANES]
    whole_ref[...] = line_ref[...].astype(BF16)
    copies = [
        pltpu.make_async_copy(whole_ref, out_hbm.at[peer], sems.at[peer])
        for peer in range(peers)
    ]
    for copy in copies:
        copy.start()
    for copy in copies:
        copy.wait()


def col_kernel(peers, k_ref, sums_ref, mass_ref, out_ref, scaling_ref):
    scaling = mass_ref[...] / jnp.sum(sums_ref[...].astype(F32), 0)
    scaling_ref[...] = scaling.astype(BF16).astype(F32)
    block = 256
    for first in range(0, k_ref.shape[0], block):
        acc = None
        for t in range(scaling.shape[0]):
            part = k_ref[first : first + block, t * LANES : (t + 1) * LANES].astype(F32)
            term = part * scaling_ref[t : t + 1, :]
            acc = term if acc is None else acc + term
        for part in range(0, block, LANES):
            line = jnp.sum(acc[part : part + LANES, :].T, 0, keepdims=True)
            at = (first + part) // LANES
            for peer in range(peers):
                out_ref[peer, at : at + 1, :] = line


def fate_kernel(
    k_ref, sums_ref, mass_ref, labels_ref, out_hbm, potential_ref, left_ref, wire_ref, sems
):
    scaling = mass_ref[...] / jnp.sum(sums_ref[...], 0)
    potential_ref[...] = entropy_weight * jnp.log(scaling)
    sets = lax.broadcasted_iota(jnp.int32, (SETS, LANES), 0)
    for t in range(scaling.shape[0]):
        member = labels_ref[t : t + 1, :] == sets
        left_ref[:, t * LANES : (t + 1) * LANES] = jnp.where(
            member, scaling[t : t + 1, :], 0.0
        ).astype(BF16)
    count = k_ref.shape[1]
    block = 512
    copies = []
    for first in range(0, count, block):
        result = jnp.dot(
            left_ref[...], k_ref[:, first : first + block], preferred_element_type=F32
        )
        for part in range(0, block, LANES):
            share = result[:, part : part + LANES]
            top = jnp.log2(jnp.max(share, 0, keepdims=True))
            power = jnp.clip(jnp.floor(top) + 1.0, LEAST_POWER, 127.0)
            scaled = jnp.minimum(share * jnp.exp2(15.0 - power) + 0.5, 32767.0)
            rest = jnp.broadcast_to(power, (WIRE_ROWS - SETS, LANES))
            coded = jnp.concatenate([scaled, rest], 0).astype(jnp.int32)
            peer = (first + part) // LANES
            wire_ref[peer] = coded.astype(jnp.int16)
            copies.append(
                pltpu.make_async_copy(wire_ref.at[peer], out_hbm.at[peer], sems.at[peer])
            )
            copies[-1].start()
    for copy in copies:
        copy.wait()


def last_kernel(at_ref, sums_ref, mass_ref, fates_ref, potential_ref):
    sums = jnp.zeros((SETS, LANES), F32)
    for peer in range(sums_ref.shape[0]):
        coded = sums_ref[peer].astype(jnp.int32).astype(F32)
        sums = sums + coded[0:SETS, :] * jnp.exp2(coded[SETS : SETS + 1, :] - 15.0)
    totals = jnp.sum(sums, 0, keepdims=True)
    fates_ref[...] = sums / totals
    own = mass_ref[pl.ds(at_ref[0], 1), :]
    potential_ref[...] = entropy_weight * jnp.log(own / totals)


def shape(dims, dtype=F32):
    return jax.ShapeDtypeStruct(dims, dtype)


def call(kernel, name, outs, in_specs, scratch=(), limit=24, out_specs=None):
    return pl.pallas_call(
        kernel,
        name=name,
        out_shape=outs,
        in_specs=in_specs,
        out_specs=out_specs if out_specs is not None else tuple(VMEM for _ in outs) if isinstance(outs, tuple) else VMEM,
        scratch_shapes=scratch,
        compiler_params=pltpu.CompilerParams(vmem_limit_bytes=limit * 2**20),
    )


def diagonal_groups(row_size, col_size):
    groups = []
    for g in range(row_size):
        group = []
        for c in range(col_size):
            x = (g // 2 + c // 4) % (row_size // 2)
            core = (g % 2 + c % 4) % 2
            group.append((x * 2 + core) * col_size + c)
        groups.append(group)
    return groups


def on_device(row_size, col_size, source_pcs, target_pcs, source_mass, target_mass, source_scaling, labels):
    row_count = source_pcs.shape[0]
    col_count = target_pcs.shape[0]
    lines_r, lines_c = row_count // LANES, col_count // LANES
    source_mass = source_mass.reshape(lines_r, LANES)
    target_mass = target_mass.reshape(lines_c, LANES)
    scaling = source_scaling.reshape(lines_r, LANES)
    labels = labels.reshape(lines_c, LANES)

    x_lines, y_lines = source_pcs.T, target_pcs.T
    x_far = pltpu.with_memory_space_constraint(x_lines, pltpu.HBM)
    y_far = pltpu.with_memory_space_constraint(y_lines, pltpu.HBM)
    stats = call(
        functools.partial(stats_kernel, col_size),
        "stats",
        shape((col_size, 2, LANES)),
        [HBM] * 2,
        [
            pltpu.VMEM(x_lines.shape, BF16),
            pltpu.VMEM(y_lines.shape, BF16),
            pltpu.SemaphoreType.DMA((2, PIECES)),
        ],
    )(x_far, y_far)
    stats = lax.all_to_all(
        stats, ("row", "col"), 0, 0,
        axis_index_groups=diagonal_groups(row_size, col_size), tiled=True,
    )
    xa, ya = call(
        points_kernel,
        "points",
        (pltpu.VMEM((row_count, DEPTH), BF16), pltpu.VMEM((col_count, DEPTH), BF16)),
        [VMEM] * 2,
    )(x_lines, y_lines)
    xa = pltpu.with_memory_space_constraint(xa, pltpu.VMEM)
    ya = pltpu.with_memory_space_constraint(ya, pltpu.VMEM)
    stats = pltpu.with_memory_space_constraint(stats, pltpu.VMEM)
    repeats = col_size // row_size
    k, sums = call(
        functools.partial(
            gen_kernel,
            row_size,
            1.0 / (repeats * row_count * row_size),
            1.0 / (col_count * col_size),
        ),
        "gen",
        (pltpu.VMEM((col_count, row_count), BF16), shape((row_size, lines_c, LANES), BF16)),
        [VMEM] * 4,
        [pltpu.VMEM((lines_c, LANES), F32)],
    )(xa, ya, stats, scaling)
    k = pltpu.with_memory_space_constraint(k, pltpu.VMEM)
    sums = lax.all_to_all(sums, "row", 0, 0, tiled=True)
    scratch = [
        pltpu.VMEM((16, col_count), BF16),
        pltpu.VMEM((lines_r, LANES), F32),
        pltpu.VMEM((lines_r, LANES), BF16),
        pltpu.SemaphoreType.DMA((col_size,)),
    ]
    sums = call(
        functools.partial(row_kernel, col_size),
        "rows",
        shape((col_size, lines_r, LANES), BF16),
        [VMEM] * 3,
        scratch,
        out_specs=HBM,
    )(k, sums, target_mass)
    sums = lax.all_to_all(sums, "col", 0, 0, tiled=True)
    scratch = [pltpu.VMEM((lines_r, LANES), F32)]
    sums = call(
        functools.partial(col_kernel, row_size),
        "cols",
        shape((row_size, lines_c, LANES)),
        [VMEM] * 3,
        scratch,
    )(k, sums, source_mass)
    sums = lax.all_to_all(sums, "row", 0, 0, tiled=True)
    sums, target_potential = call(
        fate_kernel,
        "fate",
        (shape((lines_r, WIRE_ROWS, LANES), jnp.int16), shape((lines_c, LANES))),
        [VMEM] * 4,
        [
            pltpu.VMEM((SETS, col_count), BF16),
            pltpu.VMEM((lines_r, WIRE_ROWS, LANES), jnp.int16),
            pltpu.SemaphoreType.DMA((lines_r,)),
        ],
        out_specs=(HBM, VMEM),
    )(k, sums, target_mass, labels)
    sums = lax.all_to_all(sums, "col", 0, 0, tiled=True)
    at = lax.axis_index("col").astype(jnp.int32).reshape(1)
    fates, source_potential = call(
        last_kernel,
        "last",
        (shape((SETS, LANES)), shape((1, LANES))),
        [SMEM, VMEM, VMEM],
    )(at, sums, source_mass)
    return fates.T, source_potential.reshape(LANES), target_potential.reshape(col_count)


def solution(mesh):
    placed = (P("row", None), P("col", None), P("row"), P("col"), P("row"), P("col"))
    return jax.shard_map(
        functools.partial(on_device, mesh.shape["row"], mesh.shape["col"]),
        mesh=mesh,
        in_specs=placed,
        out_specs=(P(("row", "col"), None), P(("row", "col")), P("col")),
        check_vma=False,
    )
```

```python
import functools

import jax
import jax.numpy as jnp
import numpy as np
from jax import lax
from jax.experimental import pallas as pl
from jax.experimental.pallas import tpu as pltpu
from jax.sharding import PartitionSpec as P

SETS = 32
PCS = 64
LANES = 128
DEPTH = 128
WIRE_ROWS = 40
LEAST_POWER = -111.0
entropy_weight = 0.5
offset_small = 1e-06
LOG2E = 1.4426950408889634
F32 = jnp.float32
BF16 = jnp.bfloat16
NT_DIMS = (((1,), (1,)), ((), ()))
VMEM = pl.BlockSpec(memory_space=pltpu.VMEM)
SMEM = pl.BlockSpec(memory_space=pltpu.SMEM)


def split3(t):
    hi = t.astype(BF16).astype(F32)
    mid = (t - hi).astype(BF16).astype(F32)
    lo = t - hi - mid
    return hi, mid, lo


def stats_kernel(peers, x_hbm, y_hbm, out_ref, x_ref, y_ref, sems):
    copies = [
        pltpu.make_async_copy(x_hbm, x_ref, sems.at[0]),
        pltpu.make_async_copy(y_hbm, y_ref, sems.at[1]),
    ]
    for copy in copies:
        copy.start()
    for which, in_ref in enumerate((x_ref, y_ref)):
        copies[which].wait()
        total = jnp.zeros((PCS, LANES), F32)
        squares = jnp.zeros((PCS, LANES), F32)
        for first in range(0, in_ref.shape[1], LANES):
            wide = in_ref[:, first : first + LANES].astype(F32)
            total = total + wide
            squares = squares + wide * wide
        sq = jnp.sum(squares, 0, keepdims=True)
        rest = jnp.broadcast_to(sq, (LANES - PCS, LANES))
        line = jnp.sum(jnp.concatenate([total, rest], 0).T, 0, keepdims=True)
        for peer in range(peers):
            out_ref[peer, which : which + 1, :] = line


def points_kernel(x_ref, y_ref, xa_ref, ya_ref):
    width = 512
    row = lax.broadcasted_iota(jnp.int32, (16, width), 0)
    for which, (in_ref, out_ref) in enumerate(((x_ref, xa_ref), (y_ref, ya_ref))):
        base = 3 * which
        for first in range(0, in_ref.shape[1], width):
            wide = in_ref[:, first : first + width].astype(F32)
            parts = split3(-0.5 * jnp.sum(wide * wide, 0, keepdims=True))
            extra = jnp.where((row >= 3 - base) & (row < 6 - base), 1.0, 0.0)
            for k in range(3):
                extra = jnp.where(row == base + k, parts[k], extra)
            pad = jnp.zeros((DEPTH - PCS - 16, width), F32)
            whole = jnp.concatenate([wide, extra, pad], 0)
            for part in range(0, width, LANES):
                out_ref[first + part : first + part + LANES, :] = whole[
                    :, part : part + LANES
                ].T.astype(BF16)


def gen_kernel(peers, weight_x, weight_y, xa_ref, ya_ref, stats_ref, scaling_ref, k_ref, out_ref, line_ref):
    row_count, col_count = xa_ref.shape[0], ya_ref.shape[0]
    sums = jnp.sum(stats_ref[...], 0)
    mean_x = sums[0:1, :] * weight_x
    mean_y = sums[1:2, :] * weight_y
    lane = lax.broadcasted_iota(jnp.int32, (1, LANES), 1)
    square = jnp.where(lane == PCS, mean_x + mean_y, 0.0)
    cross = jnp.where(lane < PCS, mean_x * mean_y, 0.0)
    mean_square = jnp.sum(square - 2.0 * cross, 1, keepdims=True) + offset_small
    factor = (2.0 * LOG2E) / (entropy_weight * mean_square)
    block_cols, block_rows = 2048, 256

    def one_block(index, carry):
        first = pl.multiple_of(index * block_cols, block_cols)
        acc = None
        for row in range(0, row_count, block_rows):
            inner = lax.dot_general(
                ya_ref[pl.ds(first, block_cols), :],
                xa_ref[row : row + block_rows, :],
                NT_DIMS,
                preferred_element_type=F32,
            )
            value = jnp.exp2(inner * factor)
            k_ref[pl.ds(first, block_cols), row : row + block_rows] = value.astype(BF16)
            for part in range(0, block_rows, LANES):
                at = (row + part) // LANES
                scaled = scaling_ref[at : at + 1, :].astype(BF16).astype(F32)
                term = value[:, part : part + LANES] * scaled
                acc = term if acc is None else acc + term
        for part in range(0, block_cols, LANES):
            line = jnp.sum(acc[part : part + LANES, :].T, 0, keepdims=True)
            line_ref[pl.ds(index * (block_cols // LANES) + part // LANES, 1), :] = line
        return carry

    lax.fori_loop(0, col_count // block_cols, one_block, 0, unroll=2)
    whole = line_ref[...].astype(out_ref.dtype)
    for peer in range(peers):
        out_ref[peer] = whole


def spread(ref, values):
    for t in range(values.shape[0]):
        ref[:, t * LANES : (t + 1) * LANES] = jnp.broadcast_to(
            values[t : t + 1, :], (ref.shape[0], LANES)
        ).astype(BF16)


def row_kernel(peers, k_ref, sums_ref, mass_ref, out_ref, left_ref, line_ref):
    spread(left_ref, mass_ref[...] / jnp.sum(sums_ref[...].astype(F32), 0))
    count = k_ref.shape[1]
    block = 1024
    for first in range(0, count, block):
        result = jnp.dot(
            left_ref[...], k_ref[:, first : first + block], preferred_element_type=F32
        )
        for part in range(0, block, LANES):
            at = (first + part) // LANES
            line_ref[at : at + 1, :] = result[0:1, part : part + LANES]
    whole = line_ref[...].astype(out_ref.dtype)
    for peer in range(peers):
        out_ref[peer] = whole


def col_kernel(peers, k_ref, sums_ref, mass_ref, out_ref, scaling_ref):
    scaling = mass_ref[...] / jnp.sum(sums_ref[...].astype(F32), 0)
    scaling_ref[...] = scaling.astype(BF16).astype(F32)
    block = 256
    for first in range(0, k_ref.shape[0], block):
        acc = None
        for t in range(scaling.shape[0]):
            part = k_ref[first : first + block, t * LANES : (t + 1) * LANES].astype(F32)
            term = part * scaling_ref[t : t + 1, :]
            acc = term if acc is None else acc + term
        for part in range(0, block, LANES):
            line = jnp.sum(acc[part : part + LANES, :].T, 0, keepdims=True)
            at = (first + part) // LANES
            for peer in range(peers):
                out_ref[peer, at : at + 1, :] = line


def fate_kernel(k_ref, sums_ref, mass_ref, labels_ref, out_ref, potential_ref, left_ref):
    scaling = mass_ref[...] / jnp.sum(sums_ref[...], 0)
    potential_ref[...] = entropy_weight * jnp.log(scaling)
    sets = lax.broadcasted_iota(jnp.int32, (SETS, LANES), 0)
    for t in range(scaling.shape[0]):
        member = labels_ref[t : t + 1, :] == sets
        left_ref[:, t * LANES : (t + 1) * LANES] = jnp.where(
            member, scaling[t : t + 1, :], 0.0
        ).astype(BF16)
    count = k_ref.shape[1]
    block = 1024
    for first in range(0, count, block):
        result = jnp.dot(
            left_ref[...], k_ref[:, first : first + block], preferred_element_type=F32
        )
        for part in range(0, block, LANES):
            share = result[:, part : part + LANES]
            top = jnp.log2(jnp.max(share, 0, keepdims=True))
            power = jnp.clip(jnp.floor(top) + 1.0, LEAST_POWER, 127.0)
            scaled = jnp.minimum(share * jnp.exp2(15.0 - power) + 0.5, 32767.0)
            rest = jnp.broadcast_to(power, (WIRE_ROWS - SETS, LANES))
            coded = jnp.concatenate([scaled, rest], 0).astype(jnp.int32)
            out_ref[(first + part) // LANES] = coded.astype(jnp.int16)


def last_kernel(at_ref, sums_ref, mass_ref, fates_ref, potential_ref):
    sums = jnp.zeros((SETS, LANES), F32)
    for peer in range(sums_ref.shape[0]):
        coded = sums_ref[peer].astype(jnp.int32).astype(F32)
        sums = sums + coded[0:SETS, :] * jnp.exp2(coded[SETS : SETS + 1, :] - 15.0)
    totals = jnp.sum(sums, 0, keepdims=True)
    fates_ref[...] = sums / totals
    own = mass_ref[pl.ds(at_ref[0], 1), :]
    potential_ref[...] = entropy_weight * jnp.log(own / totals)


def shape(dims, dtype=F32):
    return jax.ShapeDtypeStruct(dims, dtype)


def call(kernel, name, outs, in_specs, scratch=(), limit=24):
    return pl.pallas_call(
        kernel,
        name=name,
        out_shape=outs,
        in_specs=in_specs,
        out_specs=tuple(VMEM for _ in outs) if isinstance(outs, tuple) else VMEM,
        scratch_shapes=scratch,
        compiler_params=pltpu.CompilerParams(vmem_limit_bytes=limit * 2**20),
    )


def diagonal_groups(row_size, col_size):
    groups = []
    for g in range(row_size):
        group = []
        for c in range(col_size):
            x = (g // 2 + c // 4) % (row_size // 2)
            core = (g % 2 + c % 4) % 2
            group.append((x * 2 + core) * col_size + c)
        groups.append(group)
    return groups


def on_device(row_size, col_size, source_pcs, target_pcs, source_mass, target_mass, source_scaling, labels):
    row_count = source_pcs.shape[0]
    col_count = target_pcs.shape[0]
    lines_r, lines_c = row_count // LANES, col_count // LANES
    source_mass = source_mass.reshape(lines_r, LANES)
    target_mass = target_mass.reshape(lines_c, LANES)
    scaling = source_scaling.reshape(lines_r, LANES)
    labels = labels.reshape(lines_c, LANES)

    x_lines, y_lines = source_pcs.T, target_pcs.T
    x_far = pltpu.with_memory_space_constraint(x_lines, pltpu.HBM)
    y_far = pltpu.with_memory_space_constraint(y_lines, pltpu.HBM)
    stats = call(
        functools.partial(stats_kernel, col_size),
        "stats",
        shape((col_size, 2, LANES)),
        [pl.BlockSpec(memory_space=pltpu.HBM)] * 2,
        [
            pltpu.VMEM(x_lines.shape, BF16),
            pltpu.VMEM(y_lines.shape, BF16),
            pltpu.SemaphoreType.DMA((2,)),
        ],
    )(x_far, y_far)
    stats = lax.all_to_all(
        stats, ("row", "col"), 0, 0,
        axis_index_groups=diagonal_groups(row_size, col_size), tiled=True,
    )
    xa, ya = call(
        points_kernel,
        "points",
        (pltpu.VMEM((row_count, DEPTH), BF16), pltpu.VMEM((col_count, DEPTH), BF16)),
        [VMEM] * 2,
    )(x_lines, y_lines)
    xa = pltpu.with_memory_space_constraint(xa, pltpu.VMEM)
    ya = pltpu.with_memory_space_constraint(ya, pltpu.VMEM)
    stats = pltpu.with_memory_space_constraint(stats, pltpu.VMEM)
    repeats = col_size // row_size
    k, sums = call(
        functools.partial(
            gen_kernel,
            row_size,
            1.0 / (repeats * row_count * row_size),
            1.0 / (col_count * col_size),
        ),
        "gen",
        (pltpu.VMEM((col_count, row_count), BF16), shape((row_size, lines_c, LANES), BF16)),
        [VMEM] * 4,
        [pltpu.VMEM((lines_c, LANES), F32)],
    )(xa, ya, stats, scaling)
    k = pltpu.with_memory_space_constraint(k, pltpu.VMEM)
    sums = lax.all_to_all(sums, "row", 0, 0, tiled=True)
    scratch = [pltpu.VMEM((16, col_count), BF16), pltpu.VMEM((lines_r, LANES), F32)]
    sums = call(
        functools.partial(row_kernel, col_size),
        "rows",
        shape((col_size, lines_r, LANES), BF16),
        [VMEM] * 3,
        scratch,
    )(k, sums, target_mass)
    sums = lax.all_to_all(sums, "col", 0, 0, tiled=True)
    scratch = [pltpu.VMEM((lines_r, LANES), F32)]
    sums = call(
        functools.partial(col_kernel, row_size),
        "cols",
        shape((row_size, lines_c, LANES)),
        [VMEM] * 3,
        scratch,
    )(k, sums, source_mass)
    sums = lax.all_to_all(sums, "row", 0, 0, tiled=True)
    sums, target_potential = call(
        fate_kernel,
        "fate",
        (shape((lines_r, WIRE_ROWS, LANES), jnp.int16), shape((lines_c, LANES))),
        [VMEM] * 4,
        [pltpu.VMEM((SETS, col_count), BF16)],
    )(k, sums, target_mass, labels)
    sums = lax.all_to_all(sums, "col", 0, 0, tiled=True)
    at = lax.axis_index("col").astype(jnp.int32).reshape(1)
    fates, source_potential = call(
        last_kernel,
        "last",
        (shape((SETS, LANES)), shape((1, LANES))),
        [SMEM, VMEM, VMEM],
    )(at, sums, source_mass)
    return fates.T, source_potential.reshape(LANES), target_potential.reshape(col_count)


def solution(mesh):
    placed = (P("row", None), P("col", None), P("row"), P("col"), P("row"), P("col"))
    return jax.shard_map(
        functools.partial(on_device, mesh.shape["row"], mesh.shape["col"]),
        mesh=mesh,
        in_specs=placed,
        out_specs=(P(("row", "col"), None), P(("row", "col")), P("col")),
        check_vma=False,
    )
```
